256 devices in a mesh: src: 32 (over z, x), tgt: 8 (over y, core).
Axes of the slice: x: 4, y: 4, z: 8, core: 2. Of those that a mesh axis runs over, the one named last changes fastest.
Arguments:
- src_embed: float32 [65536, 256], P(('src', 'tgt')), may hold values from -7.5 to 7.5
- tgt_embed: float32 [32768, 256], P(('tgt', 'src')), may hold values from -7.5 to 7.5
- log_src: float32 [65536], P('src'), may hold values from -1.25 to 2.35
- log_tgt: float32 [32768], P('tgt'), may hold values from -1.25 to 2.35
- tgt_pot: float32 [32768], P('tgt'), may hold values from -1 to 6
Outputs:
- src_dual: float32 [65536], P('src')
- tgt_dual: float32 [32768], P('tgt')
The draws below stay inside these ranges and needn't reach their ends.
All inputs are finite; a program needn't handle non-finite values.
Results may differ from the reference program's by a relative error of at most 0.0003.
Values sent between devices are 32-bit elements; how exact they have to be, the bound alone decides.
No kernel may reach another device: no remote copies, remote signals or barrier semaphores. Data moves between devices by JAX's collectives and lax.ppermute only.
A program may use at most 128 MiB of HBM per device.

```python
import math
import jax
import jax.numpy as jnp
from jax import lax

E = 256
COL_DEV = 4096
ITERS = 1
NS = 65536
NT = 32768


def draw_src_embed(key, part):
    main_key = jax.random.fold_in(key, 1)
    values = jnp.clip(jax.random.normal(main_key, (NS, E), jnp.float32), -4.0, 4.0)
    return values


def draw_tgt_embed(key, part):
    main_key = jax.random.fold_in(key, 2)
    values = jnp.clip(jax.random.normal(main_key, (NT, E), jnp.float32), -4.0, 4.0)
    return values


def mass_draw(key, count):
    ramp = jnp.log1p(2.0 * jnp.arange(count, dtype=jnp.float32) / count)
    noise = jax.random.uniform(key, (count,), jnp.float32, -1.2, 1.2)
    return noise + ramp


def draw_log_src(key, part):
    return mass_draw(jax.random.fold_in(key, 21), NS)


def draw_log_tgt(key, part):
    return mass_draw(jax.random.fold_in(key, 22), NT)


def draw_tgt_pot(key, part):
    own_key = jax.random.fold_in(key, 31)
    position = (jnp.arange(NT, dtype=jnp.int32) % COL_DEV).astype(jnp.float32) / COL_DEV
    noise = jax.random.uniform(own_key, (NT,), jnp.float32, -0.4, 0.4)
    values = jnp.clip(-1.0 + 7.0 * position + noise, -1.0, 6.0)
    return values


def setup_inputs(seed: int = 0) -> dict:
    key_list = jax.random.split(jax.random.key(seed), 6)
    src_embed = draw_src_embed(jax.random.fold_in(key_list[5], 71), 0)
    tgt_embed = draw_tgt_embed(jax.random.fold_in(key_list[5], 71), 0)
    log_src = draw_log_src(jax.random.fold_in(key_list[5], 71), 0)
    log_tgt = draw_log_tgt(jax.random.fold_in(key_list[5], 71), 0)
    tgt_pot = draw_tgt_pot(jax.random.fold_in(key_list[5], 71), 0)
    return dict(src_embed=src_embed, tgt_embed=tgt_embed, log_src=log_src, log_tgt=log_tgt, tgt_pot=tgt_pot)


EPSILON = 0.05


def reference(src_embed, tgt_embed, log_src, log_tgt, tgt_pot):
    block_rows = math.gcd(NS, 1024)
    block_count = NS // block_rows
    tgt_norm = jnp.sum(tgt_embed * tgt_embed, axis=1)
    tgt_dual = tgt_pot
    src_dual = jnp.zeros((NS,), jnp.float32)
    for turn in range(ITERS):
        def sweep(carry, index):
            highest, totals = carry
            first = (index * block_rows).astype(jnp.int32)
            rows = lax.dynamic_slice_in_dim(src_embed, first, block_rows, 0)
            masses = lax.dynamic_slice_in_dim(log_src, first, block_rows, 0)
            src_norm = jnp.sum(rows * rows, axis=1)
            inner = jnp.dot(rows, tgt_embed.T, precision=lax.Precision.HIGHEST, preferred_element_type=jnp.float32)
            cost = (src_norm[:, None] + tgt_norm[None, :] - 2.0 * inner) / E
            scores = log_tgt[None, :] + (tgt_dual[None, :] - cost) / EPSILON
            row_top = jnp.max(scores, axis=1)
            row_sum = jnp.sum(jnp.exp(scores - row_top[:, None]), axis=1)
            dual_block = -EPSILON * (row_top + jnp.log(row_sum))
            column = masses[:, None] + (dual_block[:, None] - cost) / EPSILON
            column_top = jnp.maximum(highest, jnp.max(column, axis=0))
            totals = totals * jnp.exp(highest - column_top) + jnp.sum(jnp.exp(column - column_top[None, :]), axis=0)
            return (column_top, totals), dual_block

        start = (jnp.full((NT,), -jnp.inf, jnp.float32), jnp.zeros((NT,), jnp.float32))
        (column_top, totals), blocks = lax.scan(sweep, start, jnp.arange(block_count, dtype=jnp.int32))
        src_dual = blocks.reshape(NS)
        tgt_dual = -EPSILON * (column_top + jnp.log(totals))
    return src_dual, tgt_dual
```

```python
import functools
import math

import jax
import jax.numpy as jnp
from jax import lax
from jax.experimental import pallas as pl
from jax.experimental.pallas import tpu as pltpu
from jax.sharding import Mesh
from jax.sharding import PartitionSpec as P

EPSILON = 0.05
LOG2E = math.log2(math.e)
LN2 = math.log(2.0)
ZN, XN, YN, CN = 8, 4, 4, 2
VMEM = pl.BlockSpec(memory_space=pltpu.VMEM)


def shift(value, axis, size, back):
    return lax.ppermute(value, axis, [(i, (i - back) % size) for i in range(size)])


def split(value):
    high = value.astype(jnp.bfloat16)
    return high, (value - high.astype(jnp.float32)).astype(jnp.bfloat16)


def nt_dot(left, right):
    return lax.dot_general(left, right, (((1,), (1,)), ((), ())), preferred_element_type=jnp.float32)


def to_column(row):
    return jnp.transpose(jnp.broadcast_to(row, (128, 128)))


def to_row(column):
    return jnp.transpose(jnp.broadcast_to(column, (128, 128)))[0:1, :]


def pack_source_kernel(width, own_ref, other_ref, s_ref, norm_ref):
    y, core = lax.axis_index("y"), lax.axis_index("c")
    scale = 2.0 * LOG2E / (width * EPSILON)
    for ref, side in ((own_ref, core), (other_ref, 1 - core)):
        for m in range(YN):
            rows = ref[m * 256:(m + 1) * 256, :]
            place = lax.rem(y + m, YN) * 2 + side
            high, low = split(rows * scale)
            where = pl.ds(pl.multiple_of(place * 256, 256), 256)
            s_ref[where, 0:256] = high
            s_ref[where, 256:512] = low
            s_ref[where, 512:768] = high
            norm = jnp.sum(rows * rows, axis=1, keepdims=True)
            for h in range(2):
                norm_ref[pl.ds(place * 2 + h, 1), :] = to_row(norm[h * 128:(h + 1) * 128, :])


def row_pass_kernel(width, offsets, first, copies, *refs):
    count = len(offsets)
    s_ref, log_ref, pot_ref = refs[:3]
    refs = refs[3:]
    if not first:
        before_ref, refs = refs[0], refs[1:]
    *t_refs, t_out, tnorm_out, lse_out, col_ref = refs
    z, x = lax.axis_index("z"), lax.axis_index("x")
    start = 0
    for ref in t_refs:
        for b in range(ref.shape[0] // 128):
            at = slice(start * 128, (start + 1) * 128)
            t = ref[b * 128:(b + 1) * 128, :]
            high, low = split(t)
            t_out[at, 0:256] = high
            t_out[at, 256:512] = high
            t_out[at, 512:768] = low
            norm = jnp.sum(t * t, axis=1, keepdims=True)
            row = to_row(norm)
            tnorm_out[start:start + 1, :] = row
            k, m = offsets[start]
            place = lax.rem(z + k, ZN) * XN + lax.rem(x + m, XN)
            term = log_ref[pl.ds(place, 1), :] + (pot_ref[pl.ds(place, 1), :] - row / width) / EPSILON
            col_ref[at, :] = to_column(term * LOG2E)
            start += 1

    def tile(i, carry):
        s = s_ref[pl.ds(pl.multiple_of(i * 256, 256), 256), :]
        u = nt_dot(t_out[...], s)
        for h in range(2):
            v = (u[:, h * 128:(h + 1) * 128] + col_ref[...]).reshape(count * 16, 8, 128)
            top = jnp.max(jnp.max(v, axis=0), axis=0, keepdims=True)
            total = jnp.sum(jnp.sum(jnp.exp2(v - top[None]), axis=0), axis=0, keepdims=True)
            if not first:
                old = before_ref[pl.ds(2 * i + h, 1), :]
                new_top = jnp.maximum(top, old)
                total = total * jnp.exp2(top - new_top) + jnp.exp2(old - new_top)
                top = new_top
            lse = top + jnp.log2(total)
            if copies:
                for r in range(copies):
                    lse_out[r, pl.ds(2 * i + h, 1), :] = lse
            else:
                lse_out[pl.ds(2 * i + h, 1), :] = lse
        return carry

    lax.fori_loop(0, s_ref.shape[0] // 256, tile, 0)


def column_pass_kernel(width, offsets, copies, *refs):
    chunks = len(offsets)
    lse_ref, log_ref, norm_ref, s_ref = refs[:4]
    t_refs, tnorm_refs = refs[4:4 + chunks], refs[4 + chunks:4 + 2 * chunks]
    dual_out, col_out, d_ref = refs[4 + 2 * chunks:]
    z, x = lax.axis_index("z"), lax.axis_index("x")
    parts = lse_ref[...]
    top = jnp.max(parts, axis=0)
    lse = top + jnp.log2(jnp.sum(jnp.exp2(parts - top[None]), axis=0))
    dual_out[...] = norm_ref[...] / width - (EPSILON * LN2) * lse
    shifted = log_ref[...] * LOG2E - lse
    for r in range(d_ref.shape[0] // 128):
        d_ref[r * 128:(r + 1) * 128, :] = to_column(shifted[r:r + 1, :])
    rows = s_ref.shape[0]
    for t_ref, tnorm_ref, places in zip(t_refs, tnorm_refs, offsets):
        def tile(i, carry, t_ref=t_ref, tnorm_ref=tnorm_ref, places=places):
            t = t_ref[pl.ds(pl.multiple_of(i * 256, 256), 256), :]
            u = nt_dot(s_ref[...], t)
            k = jnp.int32(places[0][0]) if len(places) == 4 else jnp.where(i < 2, places[0][0], places[4][0])
            for h in range(2):
                v = (u[:, h * 128:(h + 1) * 128] + d_ref[...]).reshape(rows // 8, 8, 128)
                top = jnp.max(jnp.max(v, axis=0), axis=0, keepdims=True)
                total = jnp.sum(jnp.sum(jnp.exp2(v - top[None]), axis=0), axis=0, keepdims=True)
                lse = top + jnp.log2(total) - tnorm_ref[pl.ds(2 * i + h, 1), :] * (LOG2E / (width * EPSILON))
                m = lax.rem(2 * i + h, XN)
                place = lax.rem(z + k, ZN) * XN + lax.rem(x + m, XN)
                for r in range(copies):
                    col_out[r, pl.ds(place, 1), :] = lse
            return carry

        lax.fori_loop(0, t_ref.shape[0] // 256, tile, 0)


def join(parts):
    top = jnp.max(parts, axis=0)
    return top + jnp.log2(jnp.sum(jnp.exp2(parts - top[None]), axis=0))


def shards(src_embed, tgt_embed, log_src, log_tgt, tgt_pot):
    width = src_embed.shape[1]
    rows = log_src.shape[0]
    log_src = log_src.reshape(-1, 128)
    log_tgt = log_tgt.reshape(-1, 128)
    tgt_pot = tgt_pot.reshape(-1, 128)

    plane = jnp.concatenate([tgt_embed] + [shift(tgt_embed, "x", XN, m) for m in (1, 2, 3)])
    half = plane.shape[0] // 2
    ups, downs = [plane], [plane]
    for _ in range(3):
        ups.append(shift(ups[-1], "z", ZN, 1))
        downs.append(shift(downs[-1], "z", ZN, -1))
    far = [shift(ups[3][:half], "z", ZN, 1), shift(downs[3][half:], "z", ZN, -1)]

    column = jnp.concatenate([src_embed] + [shift(src_embed, "y", YN, m) for m in (1, 2, 3)])
    other = shift(column, "c", CN, 1)
    params = pltpu.CompilerParams(vmem_limit_bytes=60 * 2**20)
    source, src_norm = pl.pallas_call(
        functools.partial(pack_source_kernel, width),
        out_shape=(jax.ShapeDtypeStruct((rows, 3 * width), jnp.bfloat16), jax.ShapeDtypeStruct((rows // 128, 128), jnp.float32)),
        in_specs=[VMEM] * 2, out_specs=(VMEM,) * 2, compiler_params=params, name="pack",
    )(column, other)

    chunks = [[plane], [ups[1], downs[1]], [ups[2], downs[2]], [ups[3], downs[3]], far]
    four = lambda k: [(k, m) for m in range(XN)]
    offsets = [four(0), four(1) + four(7), four(2) + four(6), four(3) + four(5), four(4)]
    lse, tiles, norms = None, [], []
    for index, (chunk, places) in enumerate(zip(chunks, offsets)):
        copies = YN * CN if index == len(chunks) - 1 else 0
        count = len(places)
        inputs = [source, log_tgt, tgt_pot] + ([] if lse is None else [lse]) + chunk
        shape = (rows // 128, 128)
        t, tnorm, lse = pl.pallas_call(
            functools.partial(row_pass_kernel, width, places, lse is None, copies),
            out_shape=(
                jax.ShapeDtypeStruct((count * 128, 3 * width), jnp.bfloat16),
                jax.ShapeDtypeStruct((count, 128), jnp.float32),
                jax.ShapeDtypeStruct((copies,) + shape if copies else shape, jnp.float32),
            ),
            in_specs=[VMEM] * len(inputs), out_specs=(VMEM,) * 3,
            scratch_shapes=[pltpu.VMEM((count * 128, 128), jnp.float32)],
            compiler_params=params, name=f"row{index}",
            cost_estimate=pl.CostEstimate(flops=2 * 3 * rows * count * 128 * width, bytes_accessed=8 * 2**20, transcendentals=rows * count * 128),
        )(*inputs)
        tiles.append(t)
        norms.append(tnorm)

    parts = lax.all_to_all(lse, ("y", "c"), 0, 0, tiled=True)
    inputs = [parts, log_src, src_norm, source] + tiles + norms
    src_dual, column_lse = pl.pallas_call(
        functools.partial(column_pass_kernel, width, offsets, XN),
        out_shape=(jax.ShapeDtypeStruct((rows // 128, 128), jnp.float32), jax.ShapeDtypeStruct((XN,) + log_tgt.shape, jnp.float32)),
        in_specs=[VMEM] * len(inputs), out_specs=(VMEM,) * 2,
        scratch_shapes=[pltpu.VMEM((rows, 128), jnp.float32)],
        compiler_params=params, name="column",
    )(*inputs)
    along_x = join(lax.all_to_all(column_lse, "x", 0, 0, tiled=True))
    spread = jnp.broadcast_to(along_x[None], (ZN,) + along_x.shape)
    total = join(lax.all_to_all(spread, "z", 0, 0, tiled=True))
    return src_dual.reshape(-1), (-EPSILON * LN2 * total).reshape(-1)


def solution(mesh):
    torus = Mesh(mesh.devices.reshape(ZN, XN, YN, CN), ("z", "x", "y", "c"))
    src, tgt = ("z", "x"), ("y", "c")
    in_specs = (P(src + tgt, None), P(tgt + src, None), P(src), P(tgt), P(tgt))
    return jax.shard_map(shards, mesh=torus, in_specs=in_specs, out_specs=(P(src), P(tgt)), check_vma=False)
```

```python
import functools
import math

import jax
import jax.numpy as jnp
from jax import lax
from jax.experimental import pallas as pl
from jax.experimental.pallas import tpu as pltpu
from jax.sharding import Mesh
from jax.sharding import PartitionSpec as P


EPSILON = 0.05
LOG2E = math.log2(math.e)
LN2 = math.log(2.0)
ZN, XN, YN, CN = 8, 4, 4, 2
ROW_TILE = 256
ROW_VMEM = 8 * 2**20
VMEM = pl.BlockSpec(memory_space=pltpu.VMEM)


def shift(value, axis, size, back):
    return lax.ppermute(value, axis, [(i, (i - back) % size) for i in range(size)])


def split(value):
    high = value.astype(jnp.bfloat16)
    return high, (value - high.astype(jnp.float32)).astype(jnp.bfloat16)


def nt_dot(left, right):
    return lax.dot_general(left, right, (((1,), (1,)), ((), ())), preferred_element_type=jnp.float32)


def to_column(row):
    return jnp.transpose(jnp.broadcast_to(row, (128, 128)))


def to_row(column):
    return jnp.transpose(jnp.broadcast_to(column, (128, 128)))[0:1, :]


def pack_source_kernel(width, own_ref, other_ref, s_ref, norm_ref):
    y, core = lax.axis_index("y"), lax.axis_index("c")
    scale = 2.0 * LOG2E / (width * EPSILON)
    for ref, side in ((own_ref, core), (other_ref, 1 - core)):
        for m in range(YN):
            rows = ref[m * 256:(m + 1) * 256, :]
            place = lax.rem(y + m, YN) * 2 + side
            high, low = split(rows * scale)
            where = pl.ds(pl.multiple_of(place * 256, 256), 256)
            s_ref[where, 0:256] = high
            s_ref[where, 256:512] = low
            s_ref[where, 512:768] = high
            norm = jnp.sum(rows * rows, axis=1, keepdims=True)
            for h in range(2):
                norm_ref[pl.ds(place * 2 + h, 1), :] = to_row(norm[h * 128:(h + 1) * 128, :])


def row_pass_kernel(width, offsets, first, copies, *refs):
    count = len(offsets)
    s_ref, log_ref, pot_ref = refs[:3]
    refs = refs[3:]
    if not first:
        before_ref, refs = refs[0], refs[1:]
    *t_refs, u_out, tnorm_out, lse_out, t_scr, col_ref = refs
    z, x = lax.axis_index("z"), lax.axis_index("x")

    @pl.when(pl.program_id(0) == 0)
    def _():
        start = 0
        for ref in t_refs:
            for b in range(ref.shape[0] // 128):
                at = slice(start * 128, (start + 1) * 128)
                t = ref[b * 128:(b + 1) * 128, :]
                high, low = split(t)
                t_scr[at, 0:256] = high
                t_scr[at, 256:512] = high
                t_scr[at, 512:768] = low
                row = to_row(jnp.sum(t * t, axis=1, keepdims=True))
                tnorm_out[start:start + 1, :] = row
                k, m = offsets[start]
                place = lax.rem(z + k, ZN) * XN + lax.rem(x + m, XN)
                term = log_ref[pl.ds(place, 1), :] + (pot_ref[pl.ds(place, 1), :] - row / width) / EPSILON
                col_ref[at, :] = to_column(term * LOG2E)
                start += 1

    i = pl.program_id(0)
    tile = s_ref.shape[0]
    u = nt_dot(t_scr[...], s_ref[...])
    u_out[:, pl.ds(pl.multiple_of(i * tile, tile), tile)] = u
    for h in range(s_ref.shape[0] // 128):
        v = (u[:, h * 128:(h + 1) * 128] + col_ref[...]).reshape(count * 16, 8, 128)
        top8 = jnp.max(v, axis=0)
        top = jnp.max(top8, axis=0, keepdims=True)
        total = jnp.sum(jnp.sum(jnp.exp2(v - top[None]), axis=0), axis=0, keepdims=True)
        at = pl.ds(i * (s_ref.shape[0] // 128) + h, 1)
        if not first:
            old = before_ref[at, :]
            new_top = jnp.maximum(top, old)
            total = total * jnp.exp2(top - new_top) + jnp.exp2(old - new_top)
            top = new_top
        lse = top + jnp.log2(total)
        if copies:
            for r in range(copies):
                lse_out[r, at, :] = lse
        else:
            lse_out[at, :] = lse


def column_pass_kernel(width, offsets, copies, *refs):
    chunks = len(offsets)
    lse_refs, (log_ref, norm_ref) = refs[:YN], refs[YN:YN + 2]
    refs = refs[YN + 2:]
    tnorm_refs, u_refs = refs[:chunks], refs[chunks:2 * chunks]
    dual_out, col_out, d_ref, top_ref, total_ref = refs[2 * chunks:]
    z, x = lax.axis_index("z"), lax.axis_index("x")
    wide = u_refs[0].shape[1] // 128

    parts = jnp.stack([ref[...] for ref in lse_refs])
    lse = join(parts)
    dual_out[...] = norm_ref[...] / width - (EPSILON * LN2) * lse
    shifted = log_ref[...] * LOG2E - lse
    for r in range(wide):
        d_ref[:, r * 128:(r + 1) * 128] = jnp.broadcast_to(shifted[r:r + 1, :], (8, 128))

    def tree(op, values):
        while len(values) > 1:
            values = [op(values[k], values[k + 1]) for k in range(0, len(values), 2)]
        return values[0]

    for u_ref, tnorm_ref, places in zip(u_refs, tnorm_refs, offsets):
        def block(b, carry, u_ref=u_ref, tnorm_ref=tnorm_ref, places=places):
            for t in range(16):
                at = pl.ds(pl.multiple_of(b * 128, 128) + t * 8, 8)
                v = [u_ref[at, r * 128:(r + 1) * 128] + d_ref[:, r * 128:(r + 1) * 128] for r in range(wide)]
                top = tree(jnp.maximum, v)
                top_ref[t * 8:(t + 1) * 8, :] = top
                total_ref[t * 8:(t + 1) * 8, :] = tree(jnp.add, [jnp.exp2(e - top) for e in v])
            tops = jnp.transpose(top_ref[...])
            totals = jnp.transpose(total_ref[...])
            top = jnp.max(tops, axis=0, keepdims=True)
            total = jnp.sum(totals * jnp.exp2(tops - top), axis=0, keepdims=True)
            lse = top + jnp.log2(total) - tnorm_ref[pl.ds(b, 1), :] * (LOG2E / (width * EPSILON))
            k = jnp.where(b < XN, places[0][0], places[-1][0])
            m = lax.rem(b, XN)
            m = jnp.where(m == 2, 3, jnp.where(m == 3, 2, m))
            place = lax.rem(z + k, ZN) * XN + lax.rem(x + m, XN)
            for r in range(copies):
                col_out[r, pl.ds(place, 1), :] = lse
            return carry

        lax.fori_loop(0, u_ref.shape[0] // 128, block, 0)


def join(parts):
    top = jnp.max(parts, axis=0)
    return top + jnp.log2(jnp.sum(jnp.exp2(parts - top[None]), axis=0))


def row_pass(width, source, log_tgt, tgt_pot, lse, chunk, places, copies):
    rows, count = source.shape[0], len(places)
    shape = (rows // 128, 128)
    first = lse is None
    whole = lambda a: pl.BlockSpec(a.shape, lambda i: (0,) * a.ndim, pipeline_mode=pl.Buffered(1))
    inputs = [source, log_tgt, tgt_pot] + ([] if first else [lse]) + chunk
    specs = [pl.BlockSpec((ROW_TILE, 3 * width), lambda i: (i, 0)), whole(log_tgt), whole(tgt_pot)]
    if not first:
        specs += [whole(lse)]
    specs += [whole(c) for c in chunk]
    lse_shape = (copies,) + shape if copies else shape
    return pl.pallas_call(
        functools.partial(row_pass_kernel, width, places, first, copies),
        grid=(rows // ROW_TILE,),
        out_shape=(
            pltpu.VMEM((count * 128, rows), jnp.float32),
            jax.ShapeDtypeStruct((count, 128), jnp.float32),
            jax.ShapeDtypeStruct(lse_shape, jnp.float32),
        ),
        in_specs=specs,
        out_specs=(
            VMEM,
            pl.BlockSpec((count, 128), lambda i: (0, 0)),
            pl.BlockSpec(lse_shape, lambda i: (0,) * len(lse_shape)),
        ),
        scratch_shapes=[pltpu.VMEM((count * 128, 3 * width), jnp.bfloat16), pltpu.VMEM((count * 128, 128), jnp.float32)],
        compiler_params=pltpu.CompilerParams(vmem_limit_bytes=ROW_VMEM),
        cost_estimate=pl.CostEstimate(flops=2 * 3 * rows * count * 128 * width, bytes_accessed=4 * rows * count * 128, transcendentals=rows * count * 128),
    )(*inputs)


def column_pass(width, parts, log_src, src_norm, tgt_norms, products, offsets):
    out = (XN, sum(map(len, offsets)), 128)
    rows = log_src.size
    inputs = [*parts, log_src, src_norm, *tgt_norms, *products]
    size = rows * out[1] * 128
    return pl.pallas_call(
        functools.partial(column_pass_kernel, width, offsets, XN),
        out_shape=(jax.ShapeDtypeStruct(log_src.shape, jnp.float32), jax.ShapeDtypeStruct(out, jnp.float32)),
        in_specs=[VMEM] * len(inputs), out_specs=(VMEM,) * 2,
        scratch_shapes=[pltpu.VMEM((8, rows), jnp.float32), pltpu.VMEM((128, 128), jnp.float32), pltpu.VMEM((128, 128), jnp.float32)],
        compiler_params=pltpu.CompilerParams(vmem_limit_bytes=4 * 2**20), name="column",
        cost_estimate=pl.CostEstimate(flops=8 * size, bytes_accessed=4 * size, transcendentals=size),
    )(*inputs)


def step(src_embed, tgt_embed, log_src, log_tgt, tgt_pot):
    width = src_embed.shape[1]
    rows = log_src.shape[0]
    log_src = log_src.reshape(-1, 128)
    log_tgt = log_tgt.reshape(-1, 128)
    tgt_pot = tgt_pot.reshape(-1, 128)

    plane = jnp.concatenate([tgt_embed] + [shift(tgt_embed, "x", XN, m) for m in (1, 3, 2)])
    around = (0, 1, 3, 2)
    half = plane.shape[0] // 2
    ups, downs = [plane], [plane]
    for _ in range(3):
        ups.append(shift(ups[-1], "z", ZN, 1))
        downs.append(shift(downs[-1], "z", ZN, -1))
    far = [shift(ups[3][:half], "z", ZN, 1), shift(downs[3][half:], "z", ZN, -1)]

    column = jnp.concatenate([src_embed] + [shift(src_embed, "y", YN, m) for m in (1, 2, 3)])
    other = shift(column, "c", CN, 1)
    source, src_norm = pl.pallas_call(
        functools.partial(pack_source_kernel, width),
        out_shape=(jax.ShapeDtypeStruct((rows, 3 * width), jnp.bfloat16), jax.ShapeDtypeStruct((rows // 128, 128), jnp.float32)),
        in_specs=[VMEM] * 2, out_specs=(VMEM,) * 2, compiler_params=pltpu.CompilerParams(vmem_limit_bytes=8 * 2**20), name="pack",
        cost_estimate=pl.CostEstimate(flops=2**23, bytes_accessed=2**23, transcendentals=0),
    )(column, other)

    chunks = [[plane], [ups[1], downs[1]], [ups[2], downs[2]], [ups[3], downs[3]], far]
    four = lambda k: [(k, m) for m in around]
    offsets = [four(0), four(1) + four(7), four(2) + four(6), four(3) + four(5), four(4)]
    lse, products, norms = None, [], []
    for chunk, places in zip(chunks, offsets):
        u, tnorm, lse = row_pass(width, source, log_tgt, tgt_pot, lse, chunk, places, 0)
        norms.append(tnorm)
        products.append(u)

    lse = join(jnp.stack([lse, shift(lse, "c", CN, 1)]))
    parts = [lse] + [shift(lse, "y", YN, m) for m in (1, 3, 2)]
    src_dual, column_lse = column_pass(width, parts, log_src, src_norm, norms, products, offsets)
    along_x = join(lax.all_to_all(column_lse, "x", 0, 0, tiled=True))
    spread = jnp.broadcast_to(along_x[None], (ZN,) + along_x.shape)
    total = join(lax.all_to_all(spread, "z", 0, 0, tiled=True))
    return src_dual.reshape(-1), (-EPSILON * LN2 * total).reshape(-1)


def solution(mesh):
    torus = Mesh(mesh.devices.reshape(ZN, XN, YN, CN), ("z", "x", "y", "c"))
    src, tgt = ("z", "x"), ("y", "c")
    in_specs = (P(src + tgt, None), P(tgt + src, None), P(src), P(tgt), P(tgt))
    return jax.shard_map(step, mesh=torus, in_specs=in_specs, out_specs=(P(src), P(tgt)), check_vma=False)
```

```python
import functools
import math

import jax
import jax.numpy as jnp
from jax import lax
from jax.experimental import pallas as pl
from jax.experimental.pallas import tpu as pltpu
from jax.sharding import Mesh
from jax.sharding import PartitionSpec as P


EPSILON = 0.05
LOG2E = math.log2(math.e)
LN2 = math.log(2.0)
ZN, XN, YN, CN = 8, 4, 4, 2
ROW_TILE = 512
ROW_VMEM = 6 * 2**20
GROUP = 4
VMEM = pl.BlockSpec(memory_space=pltpu.VMEM)


def shift(value, axis, size, back):
    return lax.ppermute(value, axis, [(i, (i - back) % size) for i in range(size)])


def split(value):
    high = value.astype(jnp.bfloat16)
    return high, (value - high.astype(jnp.float32)).astype(jnp.bfloat16)


def nt_dot(left, right):
    return lax.dot_general(left, right, (((1,), (1,)), ((), ())), preferred_element_type=jnp.float32)


def to_column(row):
    return jnp.transpose(jnp.broadcast_to(row, (128, 128)))


def to_row(column):
    return jnp.transpose(jnp.broadcast_to(column, (128, 128)))[0:1, :]


def pack_source_kernel(width, own_ref, other_ref, s_ref, norm_ref):
    y, core = lax.axis_index("y"), lax.axis_index("c")
    scale = 2.0 * LOG2E / (width * EPSILON)
    for ref, side in ((own_ref, core), (other_ref, 1 - core)):
        for m in range(YN):
            rows = ref[m * 256:(m + 1) * 256, :]
            place = lax.rem(y + m, YN) * 2 + side
            high, low = split(rows * scale)
            where = pl.ds(pl.multiple_of(place * 256, 256), 256)
            s_ref[where, 0:256] = high
            s_ref[where, 256:512] = low
            norm = jnp.sum(rows * rows, axis=1, keepdims=True)
            for h in range(2):
                norm_ref[pl.ds(place * 2 + h, 1), :] = to_row(norm[h * 128:(h + 1) * 128, :])


def row_pass_kernel(width, offsets, first, *refs):
    count = len(offsets)
    s_ref, log_ref, pot_ref = refs[:3]
    refs = refs[3:]
    if not first:
        before_ref, refs = refs[0], refs[1:]
    *t_refs, u_out, tnorm_out, lse_out, t_scr, col_ref = refs
    z, x = lax.axis_index("z"), lax.axis_index("x")
    start = 0
    for ref in t_refs:
        for b in range(ref.shape[0] // 128):
            at = slice(start * 128, (start + 1) * 128)
            t = ref[b * 128:(b + 1) * 128, :]
            high, low = split(t)
            t_scr[at, 0:256] = high
            t_scr[at, 256:512] = low
            row = to_row(jnp.sum(t * t, axis=1, keepdims=True))
            tnorm_out[start:start + 1, :] = row
            k, m = offsets[start]
            place = lax.rem(z + k, ZN) * XN + lax.rem(x + m, XN)
            term = log_ref[pl.ds(place, 1), :] + (pot_ref[pl.ds(place, 1), :] - row / width) / EPSILON
            col_ref[at, :] = to_column(term * LOG2E)
            start += 1

    def product(i):
        at = slice(i * ROW_TILE, (i + 1) * ROW_TILE)
        high, low = s_ref[at, 0:256], s_ref[at, 256:512]
        t_high, t_low = t_scr[:, 0:256], t_scr[:, 256:512]
        u_out[:, at] = nt_dot(t_high, high) + nt_dot(t_high, low) + nt_dot(t_low, high)

    def totals(i):
        for h in range(ROW_TILE // 128):
            at = i * (ROW_TILE // 128) + h
            v = (u_out[:, at * 128:(at + 1) * 128] + col_ref[...]).reshape(count * 16, 8, 128)
            top = jnp.max(jnp.max(v, axis=0), axis=0, keepdims=True)
            total = jnp.sum(jnp.sum(jnp.exp2(v - top[None]), axis=0), axis=0, keepdims=True)
            if not first:
                old = before_ref[at:at + 1, :]
                new_top = jnp.maximum(top, old)
                total = total * jnp.exp2(top - new_top) + jnp.exp2(old - new_top)
                top = new_top
            lse_out[at:at + 1, :] = top + jnp.log2(total)

    tiles = s_ref.shape[0] // ROW_TILE
    product(0)
    for i in range(1, tiles):
        product(i)
        totals(i - 1)
    totals(tiles - 1)


def column_pass_kernel(width, offsets, *refs):
    chunks = len(offsets)
    lse_refs, (log_ref, norm_ref) = refs[:YN], refs[YN:YN + 2]
    refs = refs[YN + 2:]
    tnorm_refs, u_refs = refs[:chunks], refs[chunks:2 * chunks]
    dual_out, col_out, d_ref, top_ref, total_ref = refs[2 * chunks:]
    z, x = lax.axis_index("z"), lax.axis_index("x")
    wide = u_refs[0].shape[1] // 128

    parts = jnp.stack([ref[...] for ref in lse_refs])
    lse = join(parts)
    dual_out[...] = norm_ref[...] / width - (EPSILON * LN2) * lse
    shifted = log_ref[...] * LOG2E - lse
    for r in range(wide):
        d_ref[:, r * 128:(r + 1) * 128] = jnp.broadcast_to(shifted[r:r + 1, :], (8, 128))

    def tree(op, values):
        while len(values) > 1:
            values = [op(values[k], values[k + 1]) for k in range(0, len(values), 2)]
        return values[0]

    for u_ref, tnorm_ref, places in zip(u_refs, tnorm_refs, offsets):
        def blocks(g, carry, u_ref=u_ref, tnorm_ref=tnorm_ref, places=places):
            def scan(b):
                for t in range(b * 16, (b + 1) * 16):
                    at = pl.ds(pl.multiple_of(g * GROUP * 128, 128) + t * 8, 8)
                    v = [u_ref[at, r * 128:(r + 1) * 128] + d_ref[:, r * 128:(r + 1) * 128] for r in range(wide)]
                    top = tree(jnp.maximum, v)
                    top_ref[t * 8:(t + 1) * 8, :] = top
                    total_ref[t * 8:(t + 1) * 8, :] = tree(jnp.add, [jnp.exp2(e - top) for e in v])

            def finish(b):
                tops = jnp.transpose(top_ref[b * 128:(b + 1) * 128, :])
                totals = jnp.transpose(total_ref[b * 128:(b + 1) * 128, :])
                top = jnp.max(tops, axis=0, keepdims=True)
                total = jnp.sum(totals * jnp.exp2(tops - top), axis=0, keepdims=True)
                index = g * GROUP + b
                lse = top + jnp.log2(total) - tnorm_ref[pl.ds(index, 1), :] * (LOG2E / (width * EPSILON))
                k = jnp.where(index < XN, places[0][0], places[-1][0])
                place = lax.rem(z + k, ZN) * XN + lax.rem(x + places[b % XN][1], XN)
                col_out[pl.ds(place, 1), :] = lse

            scan(0)
            for b in range(1, GROUP):
                scan(b)
                finish(b - 1)
            finish(GROUP - 1)
            return carry

        lax.fori_loop(0, u_ref.shape[0] // (GROUP * 128), blocks, 0)


def join(parts):
    top = jnp.max(parts, axis=0)
    return top + jnp.log2(jnp.sum(jnp.exp2(parts - top[None]), axis=0))


def row_pass(width, source, log_tgt, tgt_pot, lse, chunk, places):
    rows, count = source.shape[0], len(places)
    first = lse is None
    inputs = [source, log_tgt, tgt_pot] + ([] if first else [lse]) + chunk
    return pl.pallas_call(
        functools.partial(row_pass_kernel, width, places, first),
        out_shape=(
            pltpu.VMEM((count * 128, rows), jnp.float32),
            jax.ShapeDtypeStruct((count, 128), jnp.float32),
            jax.ShapeDtypeStruct((rows // 128, 128), jnp.float32),
        ),
        in_specs=[VMEM] * len(inputs), out_specs=(VMEM,) * 3,
        scratch_shapes=[pltpu.VMEM((count * 128, 2 * width), jnp.bfloat16), pltpu.VMEM((count * 128, 128), jnp.float32)],
        compiler_params=pltpu.CompilerParams(vmem_limit_bytes=ROW_VMEM),
        cost_estimate=pl.CostEstimate(flops=2 * 3 * rows * count * 128 * width, bytes_accessed=4 * rows * count * 128, transcendentals=rows * count * 128),
    )(*inputs)


def column_pass(width, parts, log_src, src_norm, tgt_norms, products, offsets):
    out = (sum(map(len, offsets)), 128)
    rows = log_src.size
    inputs = [*parts, log_src, src_norm, *tgt_norms, *products]
    size = rows * out[0] * 128
    return pl.pallas_call(
        functools.partial(column_pass_kernel, width, offsets),
        out_shape=(jax.ShapeDtypeStruct(log_src.shape, jnp.float32), jax.ShapeDtypeStruct(out, jnp.float32)),
        in_specs=[VMEM] * len(inputs), out_specs=(VMEM,) * 2,
        scratch_shapes=[pltpu.VMEM((8, rows), jnp.float32), pltpu.VMEM((GROUP * 128, 128), jnp.float32), pltpu.VMEM((GROUP * 128, 128), jnp.float32)],
        compiler_params=pltpu.CompilerParams(vmem_limit_bytes=4 * 2**20), name="column",
        cost_estimate=pl.CostEstimate(flops=8 * size, bytes_accessed=4 * size, transcendentals=size),
    )(*inputs)


def step(src_embed, tgt_embed, log_src, log_tgt, tgt_pot):
    width = src_embed.shape[1]
    rows = log_src.shape[0]
    log_src = log_src.reshape(-1, 128)
    log_tgt = log_tgt.reshape(-1, 128)
    tgt_pot = tgt_pot.reshape(-1, 128)

    plane = jnp.concatenate([tgt_embed] + [shift(tgt_embed, "x", XN, m) for m in (1, 3, 2)])
    around = (0, 1, 3, 2)
    half = plane.shape[0] // 2
    ups, downs = [plane], [plane]
    for _ in range(3):
        ups.append(shift(ups[-1], "z", ZN, 1))
        downs.append(shift(downs[-1], "z", ZN, -1))
    far = [shift(ups[3][:half], "z", ZN, 1), shift(downs[3][half:], "z", ZN, -1)]

    column = jnp.concatenate([src_embed] + [shift(src_embed, "y", YN, m) for m in (1, 2, 3)])
    other = shift(column, "c", CN, 1)
    source, src_norm = pl.pallas_call(
        functools.partial(pack_source_kernel, width),
        out_shape=(jax.ShapeDtypeStruct((rows, 2 * width), jnp.bfloat16), jax.ShapeDtypeStruct((rows // 128, 128), jnp.float32)),
        in_specs=[VMEM] * 2, out_specs=(VMEM,) * 2, compiler_params=pltpu.CompilerParams(vmem_limit_bytes=8 * 2**20), name="pack",
        cost_estimate=pl.CostEstimate(flops=2**23, bytes_accessed=2**23, transcendentals=0),
    )(column, other)

    chunks = [[plane], [ups[1], downs[1]], [ups[2], downs[2]], [ups[3], downs[3]], far]
    four = lambda k: [(k, m) for m in around]
    offsets = [four(0), four(1) + four(7), four(2) + four(6), four(3) + four(5), four(4)]
    lse, products, norms = None, [], []
    for chunk, places in zip(chunks, offsets):
        u, tnorm, lse = row_pass(width, source, log_tgt, tgt_pot, lse, chunk, places)
        norms.append(tnorm)
        products.append(u)

    lse = join(jnp.stack([lse, shift(lse, "c", CN, 1)]))
    parts = [lse] + [shift(lse, "y", YN, m) for m in (1, 3, 2)]
    src_dual, column_lse = column_pass(width, parts, log_src, src_norm, norms, products, offsets)
    along_x = join(jnp.stack([column_lse] + [shift(column_lse, "x", XN, m) for m in (1, 3, 2)]))
    spread = jnp.broadcast_to(along_x[None], (ZN,) + along_x.shape)
    total = join(lax.all_to_all(spread, "z", 0, 0, tiled=True))
    return src_dual.reshape(-1), (-EPSILON * LN2 * total).reshape(-1)


def solution(mesh):
    torus = Mesh(mesh.devices.reshape(ZN, XN, YN, CN), ("z", "x", "y", "c"))
    src, tgt = ("z", "x"), ("y", "c")
    in_specs = (P(src + tgt, None), P(tgt + src, None), P(src), P(tgt), P(tgt))
    return jax.shard_map(step, mesh=torus, in_specs=in_specs, out_specs=(P(src), P(tgt)), check_vma=False)
```

```python
import functools
import math

import jax
import jax.numpy as jnp
from jax import lax
from jax.experimental import pallas as pl
from jax.experimental.pallas import tpu as pltpu
from jax.sharding import Mesh
from jax.sharding import PartitionSpec as P


EPSILON = 0.05
LOG2E = math.log2(math.e)
LN2 = math.log(2.0)
ZN, XN, YN, CN = 8, 4, 4, 2
ROW_TILE = 512
ROW_VMEM = 6 * 2**20
GROUP = 4
VMEM = pl.BlockSpec(memory_space=pltpu.VMEM)


def shift(value, axis, size, back):
    return lax.ppermute(value, axis, [(i, (i - back) % size) for i in range(size)])


def split(value):
    high = value.astype(jnp.bfloat16)
    return high, (value - high.astype(jnp.float32)).astype(jnp.bfloat16)


def nt_dot(left, right):
    return lax.dot_general(left, right, (((1,), (1,)), ((), ())), preferred_element_type=jnp.float32)


def to_column(row):
    return jnp.transpose(jnp.broadcast_to(row, (128, 128)))


def to_row(column):
    return jnp.transpose(jnp.broadcast_to(column, (128, 128)))[0:1, :]


def pack_source_kernel(width, own_ref, other_ref, s_ref, norm_ref):
    y, core = lax.axis_index("y"), lax.axis_index("c")
    scale = 2.0 * LOG2E / (width * EPSILON)
    for ref, side in ((own_ref, core), (other_ref, 1 - core)):
        for m in range(YN):
            rows = ref[m * 256:(m + 1) * 256, :]
            place = lax.rem(y + m, YN) * 2 + side
            high, low = split(rows * scale)
            where = pl.ds(pl.multiple_of(place * 256, 256), 256)
            s_ref[where, 0:256] = high
            s_ref[where, 256:512] = low
            norm = jnp.sum(rows * rows, axis=1, keepdims=True)
            for h in range(2):
                norm_ref[pl.ds(place * 2 + h, 1), :] = to_row(norm[h * 128:(h + 1) * 128, :])


def row_pass_kernel(width, offsets, first, group, *refs):
    count = len(offsets)
    s_ref, base_ref = refs[:2]
    refs = refs[2:]
    if not first:
        before_ref, refs = refs[0], refs[1:]
    *t_refs, u_out, tnorm_out, lse_out, t_scr, col_ref = refs
    z, x = lax.axis_index("z"), lax.axis_index("x")
    start = 0
    for ref in t_refs:
        for b in range(ref.shape[0] // 128):
            at = slice(start * 128, (start + 1) * 128)
            t = ref[b * 128:(b + 1) * 128, :]
            high, low = split(t)
            t_scr[at, 0:256] = high
            t_scr[at, 256:512] = low
            row = to_row(jnp.sum(t * t, axis=1, keepdims=True))
            tnorm_out[start:start + 1, :] = row
            k, m = offsets[start]
            place = lax.rem(z + k, ZN) * XN + lax.rem(x + m, XN)
            col_ref[at, :] = to_column((base_ref[pl.ds(place, 1), :] - row / (width * EPSILON)) * LOG2E)
            start += 1

    def tiles(g, carry):
        base = g * (group * ROW_TILE) if isinstance(g, int) else pl.multiple_of(g * (group * ROW_TILE), group * ROW_TILE)

        def product(i):
            at = pl.ds(base + i * ROW_TILE, ROW_TILE)
            high, low = s_ref[at, 0:256], s_ref[at, 256:512]
            t_high, t_low = t_scr[:, 0:256], t_scr[:, 256:512]
            u_out[:, at] = nt_dot(t_high, high) + nt_dot(t_high, low) + nt_dot(t_low, high)

        def totals(i):
            for h in range(ROW_TILE // 128):
                part = i * (ROW_TILE // 128) + h
                at = pl.ds(g * (group * ROW_TILE // 128) + part, 1)
                v = (u_out[:, pl.ds(base + part * 128, 128)] + col_ref[...]).reshape(count * 16, 8, 128)
                top = jnp.max(jnp.max(v, axis=0), axis=0, keepdims=True)
                total = jnp.sum(jnp.sum(jnp.exp2(v - top[None]), axis=0), axis=0, keepdims=True)
                if not first:
                    old = before_ref[at, :]
                    new_top = jnp.maximum(top, old)
                    total = total * jnp.exp2(top - new_top) + jnp.exp2(old - new_top)
                    top = new_top
                lse_out[at, :] = top + jnp.log2(total)

        product(0)
        for i in range(1, group):
            product(i)
            totals(i - 1)
        totals(group - 1)
        return carry

    groups = s_ref.shape[0] // (group * ROW_TILE)
    if groups == 1:
        tiles(0, 0)
    else:
        lax.fori_loop(0, groups, tiles, 0)


def column_pass_kernel(width, offsets, *refs):
    chunks = len(offsets)
    lse_refs, (log_ref, norm_ref) = refs[:YN], refs[YN:YN + 2]
    refs = refs[YN + 2:]
    tnorm_refs, u_refs = refs[:chunks], refs[chunks:2 * chunks]
    dual_out, col_out, d_ref, top_ref, total_ref = refs[2 * chunks:]
    z, x = lax.axis_index("z"), lax.axis_index("x")
    wide = u_refs[0].shape[1] // 128

    parts = jnp.stack([ref[...] for ref in lse_refs])
    lse = join(parts)
    dual_out[...] = norm_ref[...] / width - (EPSILON * LN2) * lse
    shifted = log_ref[...] * LOG2E - lse
    for r in range(wide):
        d_ref[:, r * 128:(r + 1) * 128] = jnp.broadcast_to(shifted[r:r + 1, :], (8, 128))

    def tree(op, values):
        while len(values) > 1:
            values = [op(values[k], values[k + 1]) for k in range(0, len(values), 2)]
        return values[0]

    for u_ref, tnorm_ref, places in zip(u_refs, tnorm_refs, offsets):
        def blocks(g, carry, u_ref=u_ref, tnorm_ref=tnorm_ref, places=places):
            def scan(b):
                for t in range(b * 16, (b + 1) * 16):
                    at = pl.ds(pl.multiple_of(g * GROUP * 128, 128) + t * 8, 8)
                    v = [u_ref[at, r * 128:(r + 1) * 128] + d_ref[:, r * 128:(r + 1) * 128] for r in range(wide)]
                    top = tree(jnp.maximum, v)
                    top_ref[t * 8:(t + 1) * 8, :] = top
                    total_ref[t * 8:(t + 1) * 8, :] = tree(jnp.add, [jnp.exp2(e - top) for e in v])

            def finish(b):
                tops = jnp.transpose(top_ref[b * 128:(b + 1) * 128, :])
                totals = jnp.transpose(total_ref[b * 128:(b + 1) * 128, :])
                top = jnp.max(tops, axis=0, keepdims=True)
                total = jnp.sum(totals * jnp.exp2(tops - top), axis=0, keepdims=True)
                index = g * GROUP + b
                lse = top + jnp.log2(total) - tnorm_ref[pl.ds(index, 1), :] * (LOG2E / (width * EPSILON))
                k = jnp.where(index < XN, places[0][0], places[-1][0])
                place = lax.rem(z + k, ZN) * XN + lax.rem(x + places[b % XN][1], XN)
                col_out[pl.ds(place, 1), :] = lse

            scan(0)
            for b in range(1, GROUP):
                scan(b)
                finish(b - 1)
            finish(GROUP - 1)
            return carry

        lax.fori_loop(0, u_ref.shape[0] // (GROUP * 128), blocks, 0)


def join(parts):
    top = jnp.max(parts, axis=0)
    return top + jnp.log2(jnp.sum(jnp.exp2(parts - top[None]), axis=0))


def row_pass(width, source, base, lse, chunk, places, group):
    rows, count = source.shape[0], len(places)
    first = lse is None
    inputs = [source, base] + ([] if first else [lse]) + chunk
    return pl.pallas_call(
        functools.partial(row_pass_kernel, width, places, first, group),
        out_shape=(
            pltpu.VMEM((count * 128, rows), jnp.float32),
            jax.ShapeDtypeStruct((count, 128), jnp.float32),
            jax.ShapeDtypeStruct((rows // 128, 128), jnp.float32),
        ),
        in_specs=[VMEM] * len(inputs), out_specs=(VMEM,) * 3,
        scratch_shapes=[pltpu.VMEM((count * 128, 2 * width), jnp.bfloat16), pltpu.VMEM((count * 128, 128), jnp.float32)],
        compiler_params=pltpu.CompilerParams(vmem_limit_bytes=ROW_VMEM),
        cost_estimate=pl.CostEstimate(flops=2 * 3 * rows * count * 128 * width, bytes_accessed=4 * rows * count * 128, transcendentals=rows * count * 128),
    )(*inputs)


def column_pass(width, parts, log_src, src_norm, tgt_norms, products, offsets):
    out = (sum(map(len, offsets)), 128)
    rows = log_src.size
    inputs = [*parts, log_src, src_norm, *tgt_norms, *products]
    size = rows * out[0] * 128
    return pl.pallas_call(
        functools.partial(column_pass_kernel, width, offsets),
        out_shape=(jax.ShapeDtypeStruct(log_src.shape, jnp.float32), jax.ShapeDtypeStruct(out, jnp.float32)),
        in_specs=[VMEM] * len(inputs), out_specs=(VMEM,) * 2,
        scratch_shapes=[pltpu.VMEM((8, rows), jnp.float32), pltpu.VMEM((GROUP * 128, 128), jnp.float32), pltpu.VMEM((GROUP * 128, 128), jnp.float32)],
        compiler_params=pltpu.CompilerParams(vmem_limit_bytes=4 * 2**20), name="column",
        cost_estimate=pl.CostEstimate(flops=8 * size, bytes_accessed=4 * size, transcendentals=size),
    )(*inputs)


def step(src_embed, tgt_embed, log_src, log_tgt, tgt_pot):
    width = src_embed.shape[1]
    rows = log_src.shape[0]
    log_src = log_src.reshape(-1, 128)
    base = (log_tgt + tgt_pot / EPSILON).reshape(-1, 128)

    plane = jnp.concatenate([tgt_embed] + [shift(tgt_embed, "x", XN, m) for m in (1, 3, 2)])
    around = (0, 1, 3, 2)
    half = plane.shape[0] // 2
    ups, downs = [plane], [plane]
    for _ in range(3):
        ups.append(shift(ups[-1], "z", ZN, 1))
        downs.append(shift(downs[-1], "z", ZN, -1))
    far = [shift(ups[3][:half], "z", ZN, 1), shift(downs[3][half:], "z", ZN, -1)]

    column = jnp.concatenate([src_embed] + [shift(src_embed, "y", YN, m) for m in (1, 2, 3)])
    other = shift(column, "c", CN, 1)
    source, src_norm = pl.pallas_call(
        functools.partial(pack_source_kernel, width),
        out_shape=(jax.ShapeDtypeStruct((rows, 2 * width), jnp.bfloat16), jax.ShapeDtypeStruct((rows // 128, 128), jnp.float32)),
        in_specs=[VMEM] * 2, out_specs=(VMEM,) * 2, compiler_params=pltpu.CompilerParams(vmem_limit_bytes=8 * 2**20), name="pack",
        cost_estimate=pl.CostEstimate(flops=2**23, bytes_accessed=2**23, transcendentals=0),
    )(column, other)

    chunks = [[plane], [ups[1], downs[1]], [ups[2], downs[2]], [ups[3], downs[3]], far]
    four = lambda k: [(k, m) for m in around]
    offsets = [four(0), four(1) + four(7), four(2) + four(6), four(3) + four(5), four(4)]
    lse, products, norms = None, [], []
    for index, (chunk, places) in enumerate(zip(chunks, offsets)):
        u, tnorm, lse = row_pass(width, source, base, lse, chunk, places, 2 if index in (1, 2) else 4)
        norms.append(tnorm)
        products.append(u)

    lse = join(jnp.stack([lse, shift(lse, "c", CN, 1)]))
    parts = [lse] + [shift(lse, "y", YN, m) for m in (1, 3, 2)]
    src_dual, column_lse = column_pass(width, parts, log_src, src_norm, norms, products, offsets)
    along_x = join(jnp.stack([column_lse] + [shift(column_lse, "x", XN, m) for m in (1, 3, 2)]))
    spread = jnp.broadcast_to(along_x[None], (ZN,) + along_x.shape)
    total = join(lax.all_to_all(spread, "z", 0, 0, tiled=True))
    return src_dual.reshape(-1), (-EPSILON * LN2 * total).reshape(-1)


def solution(mesh):
    torus = Mesh(mesh.devices.reshape(ZN, XN, YN, CN), ("z", "x", "y", "c"))
    src, tgt = ("z", "x"), ("y", "c")
    in_specs = (P(src + tgt, None), P(tgt + src, None), P(src), P(tgt), P(tgt))
    return jax.shard_map(step, mesh=torus, in_specs=in_specs, out_specs=(P(src), P(tgt)), check_vma=False)
```

```python
import functools
import math

import jax
import jax.numpy as jnp
from jax import lax
from jax.experimental import pallas as pl
from jax.experimental.pallas import tpu as pltpu
from jax.sharding import Mesh
from jax.sharding import PartitionSpec as P


EPSILON = 0.05
LOG2E = math.log2(math.e)
LN2 = math.log(2.0)
ZN, XN, YN, CN = 8, 4, 4, 2
ROW_TILE = 512
ROW_VMEM = 6 * 2**20
GROUP = 4
VMEM = pl.BlockSpec(memory_space=pltpu.VMEM)


def shift(value, axis, size, back):
    return lax.ppermute(value, axis, [(i, (i - back) % size) for i in range(size)])


def split(value):
    high = value.astype(jnp.bfloat16)
    return high, (value - high.astype(jnp.float32)).astype(jnp.bfloat16)


def nt_dot(left, right):
    return lax.dot_general(left, right, (((1,), (1,)), ((), ())), preferred_element_type=jnp.float32)


def to_column(row):
    return jnp.transpose(jnp.broadcast_to(row, (128, 128)))


def to_row(column):
    return jnp.transpose(jnp.broadcast_to(column, (128, 128)))[0:1, :]


def pack_source_kernel(width, own_ref, other_ref, s_ref, norm_ref):
    y, core = lax.axis_index("y"), lax.axis_index("c")
    scale = 2.0 * LOG2E / (width * EPSILON)
    for ref, side in ((own_ref, core), (other_ref, 1 - core)):
        for m in range(YN):
            rows = ref[m * 256:(m + 1) * 256, :]
            place = lax.rem(y + m, YN) * 2 + side
            high, low = split(rows * scale)
            where = pl.ds(pl.multiple_of(place * 256, 256), 256)
            s_ref[where, 0:256] = high
            s_ref[where, 256:512] = low
            norm = jnp.sum(rows * rows, axis=1, keepdims=True)
            for h in range(2):
                norm_ref[pl.ds(place * 2 + h, 1), :] = to_row(norm[h * 128:(h + 1) * 128, :])


def row_pass_kernel(width, offsets, first, group, *refs):
    count = len(offsets)
    s_ref, base_ref = refs[:2]
    refs = refs[2:]
    if not first:
        before_ref, refs = refs[0], refs[1:]
    *t_refs, u_out, tnorm_out, lse_out, t_scr, col_ref = refs
    z, x = lax.axis_index("z"), lax.axis_index("x")
    start = 0
    for ref in t_refs:
        for b in range(ref.shape[0] // 128):
            at = slice(start * 128, (start + 1) * 128)
            t = ref[b * 128:(b + 1) * 128, :]
            high, low = split(t)
            t_scr[at, 0:256] = high
            t_scr[at, 256:512] = low
            row = to_row(jnp.sum(t * t, axis=1, keepdims=True))
            tnorm_out[start:start + 1, :] = row
            k, m = offsets[start]
            place = lax.rem(z + k, ZN) * XN + lax.rem(x + m, XN)
            col_ref[at, :] = to_column((base_ref[pl.ds(place, 1), :] - row / (width * EPSILON)) * LOG2E)
            start += 1

    def tiles(g, carry):
        base = g * (group * ROW_TILE) if isinstance(g, int) else pl.multiple_of(g * (group * ROW_TILE), group * ROW_TILE)

        def product(i):
            at = pl.ds(base + i * ROW_TILE, ROW_TILE)
            high, low = s_ref[at, 0:256], s_ref[at, 256:512]
            t_high, t_low = t_scr[:, 0:256], t_scr[:, 256:512]
            u_out[:, at] = nt_dot(t_high, high) + nt_dot(t_high, low) + nt_dot(t_low, high)

        def totals(i):
            for h in range(ROW_TILE // 128):
                part = i * (ROW_TILE // 128) + h
                at = pl.ds(g * (group * ROW_TILE // 128) + part, 1)
                v = (u_out[:, pl.ds(base + part * 128, 128)] + col_ref[...]).reshape(count * 16, 8, 128)
                top = jnp.max(jnp.max(v, axis=0), axis=0, keepdims=True)
                total = jnp.sum(jnp.sum(jnp.exp2(v - top[None]), axis=0), axis=0, keepdims=True)
                if not first:
                    old = before_ref[at, :]
                    new_top = jnp.maximum(top, old)
                    total = total * jnp.exp2(top - new_top) + jnp.exp2(old - new_top)
                    top = new_top
                lse_out[at, :] = top + jnp.log2(total)

        product(0)
        for i in range(1, group):
            product(i)
            totals(i - 1)
        totals(group - 1)
        return carry

    groups = s_ref.shape[0] // (group * ROW_TILE)
    if groups == 1:
        tiles(0, 0)
    else:
        lax.fori_loop(0, groups, tiles, 0)


def column_pass_kernel(width, offsets, *refs):
    chunks = len(offsets)
    lse_refs, (log_ref, norm_ref) = refs[:YN], refs[YN:YN + 2]
    refs = refs[YN + 2:]
    tnorm_refs, u_refs = refs[:chunks], refs[chunks:2 * chunks]
    dual_out, col_out, d_ref, top_ref, total_ref = refs[2 * chunks:]
    z, x = lax.axis_index("z"), lax.axis_index("x")
    wide = u_refs[0].shape[1] // 128

    parts = jnp.stack([ref[...] for ref in lse_refs])
    lse = join(parts)
    dual_out[...] = norm_ref[...] / width - (EPSILON * LN2) * lse
    shifted = log_ref[...] * LOG2E - lse
    for r in range(wide):
        d_ref[:, r * 128:(r + 1) * 128] = jnp.broadcast_to(shifted[r:r + 1, :], (8, 128))

    def tree(op, values):
        while len(values) > 1:
            values = [op(values[k], values[k + 1]) for k in range(0, len(values), 2)]
        return values[0]

    for u_ref, tnorm_ref, places in zip(u_refs, tnorm_refs, offsets):
        def blocks(g, carry, u_ref=u_ref, tnorm_ref=tnorm_ref, places=places):
            def scan(b):
                for t in range(b * 16, (b + 1) * 16):
                    at = pl.ds(pl.multiple_of(g * GROUP * 128, 128) + t * 8, 8)
                    v = [u_ref[at, r * 128:(r + 1) * 128] + d_ref[:, r * 128:(r + 1) * 128] for r in range(wide)]
                    top = tree(jnp.maximum, v)
                    top_ref[t * 8:(t + 1) * 8, :] = top
                    total_ref[t * 8:(t + 1) * 8, :] = tree(jnp.add, [jnp.exp2(e - top) for e in v])

            def finish(b):
                tops = jnp.transpose(top_ref[b * 128:(b + 1) * 128, :])
                totals = jnp.transpose(total_ref[b * 128:(b + 1) * 128, :])
                top = jnp.max(tops, axis=0, keepdims=True)
                total = jnp.sum(totals * jnp.exp2(tops - top), axis=0, keepdims=True)
                index = g * GROUP + b
                lse = top + jnp.log2(total) - tnorm_ref[pl.ds(index, 1), :] * (LOG2E / (width * EPSILON))
                k = jnp.where(index < XN, places[0][0], places[-1][0])
                place = lax.rem(z + k, ZN) * XN + lax.rem(x + places[b % XN][1], XN)
                col_out[pl.ds(place, 1), :] = lse

            scan(0)
            for b in range(1, GROUP):
                scan(b)
                finish(b - 1)
            finish(GROUP - 1)
            return carry

        lax.fori_loop(0, u_ref.shape[0] // (GROUP * 128), blocks, 0)


def join(parts):
    top = jnp.max(parts, axis=0)
    return top + jnp.log2(jnp.sum(jnp.exp2(parts - top[None]), axis=0))


def row_pass(width, source, base, lse, chunk, places, group):
    rows, count = source.shape[0], len(places)
    first = lse is None
    inputs = [source, base] + ([] if first else [lse]) + chunk
    return pl.pallas_call(
        functools.partial(row_pass_kernel, width, places, first, group),
        out_shape=(
            pltpu.VMEM((count * 128, rows), jnp.float32),
            jax.ShapeDtypeStruct((count, 128), jnp.float32),
            jax.ShapeDtypeStruct((rows // 128, 128), jnp.float32),
        ),
        in_specs=[VMEM] * len(inputs), out_specs=(VMEM,) * 3,
        scratch_shapes=[pltpu.VMEM((count * 128, 2 * width), jnp.bfloat16), pltpu.VMEM((count * 128, 128), jnp.float32)],
        compiler_params=pltpu.CompilerParams(vmem_limit_bytes=ROW_VMEM),
        cost_estimate=pl.CostEstimate(flops=2 * 3 * rows * count * 128 * width, bytes_accessed=4 * rows * count * 128, transcendentals=rows * count * 128),
    )(*inputs)


def column_pass(width, parts, log_src, src_norm, tgt_norms, products, offsets):
    out = (sum(map(len, offsets)), 128)
    rows = log_src.size
    inputs = [*parts, log_src, src_norm, *tgt_norms, *products]
    size = rows * out[0] * 128
    return pl.pallas_call(
        functools.partial(column_pass_kernel, width, offsets),
        out_shape=(jax.ShapeDtypeStruct(log_src.shape, jnp.float32), jax.ShapeDtypeStruct(out, jnp.float32)),
        in_specs=[VMEM] * len(inputs), out_specs=(VMEM,) * 2,
        scratch_shapes=[pltpu.VMEM((8, rows), jnp.float32), pltpu.VMEM((GROUP * 128, 128), jnp.float32), pltpu.VMEM((GROUP * 128, 128), jnp.float32)],
        compiler_params=pltpu.CompilerParams(vmem_limit_bytes=4 * 2**20), name="column",
        cost_estimate=pl.CostEstimate(flops=8 * size, bytes_accessed=4 * size, transcendentals=size),
    )(*inputs)


def step(src_embed, tgt_embed, log_src, log_tgt, tgt_pot):
    width = src_embed.shape[1]
    rows = log_src.shape[0]
    log_src = log_src.reshape(-1, 128)
    base = (log_tgt + tgt_pot / EPSILON).reshape(-1, 128)

    plane = jnp.concatenate([tgt_embed] + [shift(tgt_embed, "x", XN, m) for m in (1, 3, 2)])
    around = (0, 1, 3, 2)
    half = plane.shape[0] // 2
    ups, downs = [plane], [plane]
    for _ in range(2):
        ups.append(shift(ups[-1], "z", ZN, 1))
        downs.append(shift(downs[-1], "z", ZN, -1))
    third_up = [shift(part, "z", ZN, 1) for part in (ups[2][:half], ups[2][half:])]
    third_down = [shift(part, "z", ZN, -1) for part in (downs[2][:half], downs[2][half:])]
    far = [shift(third_up[0], "z", ZN, 1), shift(third_down[1], "z", ZN, -1)]

    column = jnp.concatenate([src_embed] + [shift(src_embed, "y", YN, m) for m in (1, 2, 3)])
    other = shift(column, "c", CN, 1)
    source, src_norm = pl.pallas_call(
        functools.partial(pack_source_kernel, width),
        out_shape=(jax.ShapeDtypeStruct((rows, 2 * width), jnp.bfloat16), jax.ShapeDtypeStruct((rows // 128, 128), jnp.float32)),
        in_specs=[VMEM] * 2, out_specs=(VMEM,) * 2, compiler_params=pltpu.CompilerParams(vmem_limit_bytes=8 * 2**20), name="pack",
        cost_estimate=pl.CostEstimate(flops=2**23, bytes_accessed=2**23, transcendentals=0),
    )(column, other)

    chunks = [[plane], [ups[1], downs[1]], [ups[2], downs[2]], third_up + third_down, far]
    four = lambda k: [(k, m) for m in around]
    offsets = [four(0), four(1) + four(7), four(2) + four(6), four(3) + four(5), four(4)]
    lse, products, norms = None, [], []
    for index, (chunk, places) in enumerate(zip(chunks, offsets)):
        u, tnorm, lse = row_pass(width, source, base, lse, chunk, places, 2 if index in (1, 2) else 4)
        norms.append(tnorm)
        products.append(u)

    lse = join(jnp.stack([lse, shift(lse, "c", CN, 1)]))
    parts = [lse] + [shift(lse, "y", YN, m) for m in (1, 3, 2)]
    src_dual, column_lse = column_pass(width, parts, log_src, src_norm, norms, products, offsets)
    along_x = join(jnp.stack([column_lse] + [shift(column_lse, "x", XN, m) for m in (1, 3, 2)]))
    spread = jnp.broadcast_to(along_x[None], (ZN,) + along_x.shape)
    total = join(lax.all_to_all(spread, "z", 0, 0, tiled=True))
    return src_dual.reshape(-1), (-EPSILON * LN2 * total).reshape(-1)


def solution(mesh):
    torus = Mesh(mesh.devices.reshape(ZN, XN, YN, CN), ("z", "x", "y", "c"))
    src, tgt = ("z", "x"), ("y", "c")
    in_specs = (P(src + tgt, None), P(tgt + src, None), P(src), P(tgt), P(tgt))
    return jax.shard_map(step, mesh=torus, in_specs=in_specs, out_specs=(P(src), P(tgt)), check_vma=False)
```
